32 devices in a mesh: grp: 2 (over y), gz: 4 (over z), phi: 4 (over x, core).
Axes of the slice: x: 2, y: 2, z: 4, core: 2. Of those that a mesh axis runs over, the one named last changes fastest.
Arguments:
- charge: bfloat16 [2048, 128, 256], P(('grp', 'phi'), 'gz'), parts along dimension 0, may hold values from -44 to 44
- orders: int32 [64], replicated, may hold values from 1 to 255, as said below
- electrode: int32 [128, 256], P('gz'), may hold values 0 or 1
Outputs:
- distortion: bfloat16 [2048, 128, 256], P(('grp', 'phi'), 'gz'), parts along dimension 0
- potential: float32 [256, 128, 256], P(('grp', 'phi'), 'gz'), parts along dimension 0
The draws below stay inside these ranges and needn't reach their ends.
There are 2 independent parts, one for each index of `grp`. The reference program is written for one: setup_inputs(seed, part) draws one part's arguments, and reference() takes and returns one part's arrays. A program takes and returns all parts, laid end to end along the dimension named above; an argument that names none is the same for every part. Nothing has to cross between parts.
Inputs may be any that keep to these rules, and one draw needn't show every extreme that they name: The 64 orders are distinct, and 1 and 255 are among them.
All inputs are finite; a program needn't handle non-finite values. No bound on the sum of `electrode` on one device may be relied on, other than what follows from the above.
Results may differ from the reference program's by a relative error of at most 0.0059.
Values may be sent and summed in bfloat16 or wider, within the bound.
No kernel may reach another device: no remote copies, remote signals or barrier semaphores. Data moves between devices by JAX's collectives and lax.ppermute only.
A program may use at most 64 MiB of HBM per device.

```python
import math
import jax
import jax.numpy as jnp
from jax import lax

PHI = 1024
ORDERS = 64
MODES = 128
NR = 256
SWEEPS = 4
NZ = 128
N_PHI = 4


def draw_charge(key, part):
    layers = jax.random.truncated_normal(key, -4.0, 4.0, (PHI, NZ + 1, NR), jnp.float32)
    layers = 6.0 * layers
    return (layers[:, 1:] - 0.8 * layers[:, :-1]).astype(jnp.bfloat16)


def draw_orders(key, part):
    first_key, second_key = jax.random.split(jax.random.fold_in(key, 7))
    limit = PHI // 4
    middle = jax.random.permutation(first_key, limit - 3).astype(jnp.int32) + 2
    ends = jnp.array([1, limit - 1], dtype=jnp.int32)
    values = jnp.concatenate([ends, middle[:ORDERS - 2]], 0)
    placing = jax.random.permutation(second_key, ORDERS).astype(jnp.int32)
    return jnp.take(values, placing, axis=0)


def place_ends(values, stream_key, smallest, top_value):
    shape = values.shape
    index_at = [jax.random.randint(jax.random.fold_in(stream_key, axis), (), 0, shape[axis]) for axis in range(len(shape))]
    values = values.at[tuple(index_at)].set(smallest)
    longest = shape.index(max(shape))
    index_at[longest] = (index_at[longest] + 1) % shape[longest]
    return values.at[tuple(index_at)].set(top_value)


def setup_inputs(seed: int = 0, part: int = 0) -> dict:
    key_list = jax.random.split(jax.random.key(seed), 4)
    part_keys = jax.random.split(jax.random.fold_in(key_list[3], part), 4)
    charge = draw_charge(jax.random.fold_in(jax.random.fold_in(key_list[3], part), 71), part)
    orders = draw_orders(jax.random.fold_in(key_list[3], 71), part)
    electrode = place_ends((jax.random.randint(key_list[2], (NZ, NR), 0, 16) < 1).astype(jnp.int32), jax.random.fold_in(key_list[2], 1), 0, 1)
    return dict(charge=charge, orders=orders, electrode=electrode)


def make_table(orders):
    positions = jnp.arange(PHI, dtype=jnp.int32)
    phase_int = (orders[:, None] * positions[None, :]) % PHI
    angles = phase_int.astype(jnp.float32) * (2.0 * math.pi / PHI)
    return jnp.concatenate([jnp.cos(angles), jnp.sin(angles)], 0).astype(jnp.bfloat16)


def radial_terms(order_values, radial_cells):
    radius = jnp.arange(radial_cells, dtype=jnp.float32) + (radial_cells // 2 + 0.5)
    outer_coef = 1.0 + 0.5 / radius
    inner_coef = 1.0 - 0.5 / radius
    diagonal = 4.0 + (order_values[:, None] / radius[None, :]) ** 2
    return outer_coef, inner_coef, diagonal[:, None, :]


def radial_sum(field_now, outer_coef, inner_coef):
    zero_plane = jnp.zeros_like(field_now[..., :1])
    upper_cell = jnp.concatenate([field_now[..., 1:], zero_plane], -1)
    lower_cell = jnp.concatenate([zero_plane, field_now[..., :-1]], -1)
    return outer_coef * upper_cell + inner_coef * lower_cell, upper_cell, lower_cell


def reference(charge, orders, electrode):
    basis_table = make_table(orders)
    flattened = charge.reshape(PHI, NZ * NR)
    source = jnp.dot(basis_table, flattened, preferred_element_type=jnp.float32).reshape(MODES, NZ, NR) * PHI ** -0.5
    order_values = jnp.concatenate([orders, orders]).astype(jnp.float32)
    outer_coef, inner_coef, diagonal = radial_terms(order_values, NR)
    open_cells = (1 - electrode).astype(jnp.float32)
    potential = open_cells * source / diagonal
    for sweep in range(SWEEPS):
        zero_plane = jnp.zeros_like(potential[:, :1])
        upper_plane = jnp.concatenate([potential[:, 1:], zero_plane], 1)
        lower_plane = jnp.concatenate([zero_plane, potential[:, :-1]], 1)
        radial, _, _ = radial_sum(potential, outer_coef, inner_coef)
        neighbours = upper_plane + lower_plane + radial
        potential = open_cells * (source + neighbours) / diagonal
    _, upper_cell, lower_cell = radial_sum(potential, outer_coef, inner_coef)
    radial_field = 0.5 * (upper_cell - lower_cell)
    suffix = lax.cumsum(radial_field, axis=1, reverse=True)
    mode_shift = (suffix * NZ ** -0.5).astype(jnp.bfloat16).reshape(MODES, NZ * NR)
    blocks = basis_table.T.reshape(N_PHI, PHI // N_PHI, MODES)

    def synthesize(weights):
        return (jnp.dot(weights, mode_shift, preferred_element_type=jnp.float32) * MODES ** -0.5).astype(jnp.bfloat16)

    distortion = lax.map(synthesize, blocks).reshape(PHI, NZ, NR)
    return distortion, potential
```

```python
import functools
import math

import jax
import jax.numpy as jnp
from jax import lax
from jax.experimental import pallas as pl
from jax.experimental.pallas import tpu as pltpu
from jax.sharding import PartitionSpec as P

PHI = 1024
ORDERS = 64
MODES = 128
SWEEPS = 4
TILE = 8
LANES = 128
F32 = jnp.float32
BF16 = jnp.bfloat16


def params():
    return pltpu.CompilerParams(vmem_limit_bytes=48 << 20)


def cosine(phase):
    folded = jnp.abs(jnp.bitwise_and(phase, PHI - 1) - PHI // 2)
    sign = jnp.where(folded > PHI // 4, 1.0, -1.0).astype(F32)
    near = jnp.where(folded > PHI // 4, PHI // 2 - folded, folded)
    angle = near.astype(F32) * (2.0 * math.pi / PHI)
    square = angle * angle
    total = jnp.full_like(square, 1.0 / math.factorial(14) * -1.0)
    for term in range(6, -1, -1):
        total = total * square + (-1.0) ** term / math.factorial(2 * term)
    return sign * total


def reversed_bits(count):
    order, step = [0], count
    while step > 1:
        step //= 2
        order = order + [g + step for g in order]
    return order


def roll(value, shift):
    return pltpu.roll(value, shift % value.shape[-1], value.ndim - 1)


def analyse_kernel(charge_ref, basis_ref, keep_ref, send_ref, staged):
    rows, depth, cells = charge_ref.shape
    half = keep_ref.shape[1]
    parts = range(0, cells, LANES)
    for i, lane in enumerate(parts):
        block = charge_ref[:, :, lane:lane + LANES].astype(F32)
        staged[i] = block.reshape(rows * depth, LANES)
    for z in range(depth):
        planes = [staged[i, pl.ds(z, rows, stride=depth), :] for i, _ in enumerate(parts)]
        plane = jnp.concatenate(planes, 1).astype(BF16)
        sums = jnp.dot(basis_ref[...], plane, preferred_element_type=F32)
        keep_ref[z] = sums[:half]
        send_ref[z] = sums[half:]


def analyse(charge, basis, tiles):
    rows, depth, cells = charge.shape
    modes = basis.shape[0]
    first, step = tiles[0], (tiles[1] - tiles[0] if len(tiles) > 1 else 1)
    part = jax.ShapeDtypeStruct((len(tiles) * TILE, modes // 2, cells), F32)
    out = pl.BlockSpec((TILE, modes // 2, cells), lambda i: (i, 0, 0))
    return pl.pallas_call(
        analyse_kernel,
        grid=(len(tiles),),
        in_specs=[
            pl.BlockSpec((rows, TILE, cells), lambda i: (0, first + step * i, 0)),
            pl.BlockSpec((modes, rows), lambda i: (0, 0)),
        ],
        out_specs=[out, out],
        out_shape=[part, part],
        scratch_shapes=[pltpu.VMEM((cells // LANES, rows * TILE, LANES), F32)],
        compiler_params=params(),
        name="analyse",
    )(charge, basis)


def round_kernel(order, reset, keep_ref, recv_ref, state_ref, out_ref, left_ref):
    error = state_ref[...]
    for z in order:
        if z in reset:
            error = jnp.zeros_like(error)
        exact = keep_ref[z] + recv_ref[z] + error
        rounded = exact.astype(BF16)
        out_ref[z] = rounded
        error = exact - rounded.astype(F32)
    left_ref[...] = error


def round_sums(keep, recv, state, order, reset):
    depth, modes, cells = keep.shape
    rows = modes // 2
    part = pl.BlockSpec((depth, rows, cells), lambda i: (0, 1, 0))
    flat = pl.BlockSpec((rows, cells), lambda i: (0, 0))
    return pl.pallas_call(
        functools.partial(round_kernel, order, reset),
        grid=(1,),
        in_specs=[part, part, flat],
        out_specs=[pl.BlockSpec((depth, rows, cells), lambda i: (0, 0, 0)), flat],
        out_shape=[
            jax.ShapeDtypeStruct((depth, rows, cells), BF16),
            jax.ShapeDtypeStruct((rows, cells), F32),
        ],
        compiler_params=params(),
        name="round_sums",
    )(keep, recv, state)


def solve_kernel(depth, total_depth, keep_ref, recv_ref, far_ref, before_ref, after_ref,
                 open_ref, order_ref, pot_ref, shift_ref, total_ref, src, pot, staged):
    rows, cells = before_ref.shape[1:]
    parts = range(0, cells, LANES)
    halo = SWEEPS
    column = lax.broadcasted_iota(jnp.int32, (rows, cells), 1)
    radius = column.astype(F32) + (cells // 2 + 0.5)
    outer = jnp.where(column == cells - 1, 0.0, 1.0 + 0.5 / radius)
    inner = jnp.where(column == 0, 0.0, 1.0 - 0.5 / radius)
    ratio = order_ref[...] / radius
    inverse = 1.0 / (4.0 + ratio * ratio)
    scale = PHI ** -0.5
    src[0:halo] = before_ref[...]
    src[halo + depth:] = after_ref[...]

    def gather(z, carry):
        src[z + halo] = (keep_ref[z] + recv_ref[z] + far_ref[z].astype(F32)) * scale
        return carry

    lax.fori_loop(0, depth, gather, 0, unroll=4)
    span = depth + 2 * halo

    def start(z, carry):
        pot[z] = src[z] * inverse * open_ref[pl.ds(z, 1), :]
        return carry

    lax.fori_loop(0, span, start, 0, unroll=4)

    def updated(z, here, below, above):
        radial = outer * roll(here, -1) + inner * roll(here, 1)
        return (src[z] + (below + above) + radial) * inverse * open_ref[pl.ds(z, 1), :]

    for sweep in range(1, SWEEPS):
        def step(z, below):
            here = pot[z]
            pot[z] = updated(z, here, below, pot[z + 1])
            return here

        lax.fori_loop(sweep, span - sweep, step, pot[sweep - 1], unroll=2)

    field_scale = 0.5 * total_depth ** -0.5
    upper_scale = jnp.where(column == cells - 1, 0.0, field_scale)
    lower_scale = jnp.where(column == 0, 0.0, field_scale)

    def last(i, carry):
        above, running = carry
        z = depth - 1 - i
        here = pot[z + halo]
        new = updated(z + halo, here, pot[z + halo - 1], above)
        for i, lane in enumerate(parts):
            staged[i, pl.ds(z, rows, stride=depth), :] = new[:, lane:lane + LANES]
        running = running + (upper_scale * roll(new, -1) - lower_scale * roll(new, 1))
        shift_ref[z] = running
        return here, running

    _, running = lax.fori_loop(0, depth, last, (pot[depth + halo], jnp.zeros((rows, cells), F32)), unroll=2)
    total_ref[...] = running
    for i, lane in enumerate(parts):
        pot_ref[:, :, lane:lane + LANES] = staged[i].reshape(rows, depth, LANES)


def solve(keep, recv, far, before, after, open_cells, orders, total_depth):
    depth, _, cells = keep.shape
    rows = far.shape[1]
    span = depth + 2 * SWEEPS
    half = pl.BlockSpec((depth, rows, cells), lambda i: (0, 0, 0))
    edge = pl.BlockSpec((SWEEPS, rows, cells), lambda i: (0, 0, 0))
    flat = lambda a, b: pl.BlockSpec((a, b), lambda i: (0, 0))
    return pl.pallas_call(
        functools.partial(solve_kernel, depth, total_depth),
        grid=(1,),
        in_specs=[half, half, half, edge, edge, flat(span, cells), flat(rows, 1)],
        out_specs=[pl.BlockSpec((rows, depth, cells), lambda i: (0, 0, 0)), half, flat(rows, cells)],
        out_shape=[
            jax.ShapeDtypeStruct((rows, depth, cells), F32),
            jax.ShapeDtypeStruct((depth, rows, cells), F32),
            jax.ShapeDtypeStruct((rows, cells), F32),
        ],
        scratch_shapes=[
            pltpu.VMEM((span, rows, cells), F32),
            pltpu.VMEM((span, rows, cells), F32),
            pltpu.VMEM((cells // LANES, rows * depth, LANES), F32),
        ],
        compiler_params=params(),
        name="solve",
    )(keep, recv, far, before, after, open_cells, orders)


def synthesise_kernel(count, *refs):
    pieces, weight_ref, out_ref, staged = refs[:count], refs[count], refs[count + 1], refs[count + 2]
    rows, depth, cells = out_ref.shape
    parts = range(0, cells, LANES)
    for z in range(depth):
        shifts = jnp.concatenate([piece[z] for piece in pieces], 0)
        plane = jnp.dot(weight_ref[...], shifts, preferred_element_type=F32) * MODES ** -0.5
        for i, lane in enumerate(parts):
            staged[i, pl.ds(z, rows, stride=depth), :] = plane[:, lane:lane + LANES]
    for i, lane in enumerate(parts):
        out_ref[:, :, lane:lane + LANES] = staged[i].reshape(rows, depth, LANES).astype(BF16)


def synthesise(pieces, weights):
    depth, _, cells = pieces[0].shape
    rows, modes = weights.shape
    return pl.pallas_call(
        functools.partial(synthesise_kernel, len(pieces)),
        grid=(depth // TILE,),
        in_specs=[pl.BlockSpec((TILE, piece.shape[1], cells), lambda i: (i, 0, 0)) for piece in pieces]
        + [pl.BlockSpec((rows, modes), lambda i: (0, 0))],
        out_specs=pl.BlockSpec((rows, TILE, cells), lambda i: (0, i, 0)),
        out_shape=jax.ShapeDtypeStruct((rows, depth, cells), BF16),
        scratch_shapes=[pltpu.VMEM((cells // LANES, rows * TILE, LANES), F32)],
        compiler_params=params(),
        name="synthesise",
    )(*pieces, weights)


def exchanged(block, axis, bit):
    return lax.ppermute(block, axis, [(i, i ^ bit) for i in range(lax.axis_size(axis))])


def moved(block, axis, distance):
    devices = range(lax.axis_size(axis))
    return lax.ppermute(block, axis, [(i - distance, i) for i in devices if i - distance in devices])


def later_sum(totals, axis):
    count = lax.axis_size(axis)
    if count <= 4:
        arrived = [moved(totals, axis, -d) for d in range(1, count)]
        return sum(arrived[1:], arrived[0])
    running, step = totals, 1
    while step < count:
        running = running + moved(running, axis, -step)
        step *= 2
    return moved(running, axis, -1)


def on_device(charge, orders, electrode):
    phi_rows, depth, cells = charge.shape
    devices = lax.axis_size("phi")
    mode_rows = MODES // devices
    total_depth = lax.axis_size("gz") * depth
    me = lax.axis_index("phi")
    groups = reversed_bits(devices)

    group_of_row = jnp.array([g for g in groups for _ in range(mode_rows)], jnp.int32)
    row_in_group = jnp.array([i for _ in groups for i in range(mode_rows)], jnp.int32)
    mode_ids = jnp.bitwise_xor(group_of_row, me) * mode_rows + row_in_group
    matches = mode_ids[:, None] % ORDERS == jnp.arange(ORDERS, dtype=jnp.int32)[None, :]
    row_orders = jnp.sum(jnp.where(matches, orders[None, :], 0), 1)
    quarter = jnp.where(mode_ids >= ORDERS, PHI // 4, 0)
    cells_here = me * phi_rows + jnp.arange(phi_rows, dtype=jnp.int32)
    basis = cosine(row_orders[:, None] * cells_here[None, :] - quarter[:, None]).astype(BF16)
    weights = cosine(cells_here[:, None] * row_orders[None, :] - quarter[None, :]).astype(BF16)

    open_cells = (1 - electrode).astype(F32)
    open_wide = jnp.concatenate(
        [moved(open_cells[depth - SWEEPS:], "gz", 1), open_cells, moved(open_cells[:SWEEPS], "gz", -1)], 0
    )

    keep, send = analyse(charge, basis, list(range(depth // TILE)))
    bit = 1
    recv = exchanged(send, "phi", bit)
    while bit * 4 < devices:
        bit *= 2
        half = keep.shape[1] // 2
        joined = keep + recv
        keep = joined[:, :half]
        recv = exchanged(joined[:, half:], "phi", bit)
    top = devices // 2
    state = jnp.zeros((mode_rows, cells), F32)
    far, _ = round_sums(keep, recv, state, list(range(depth - 1, -1, -1)), ())
    far = exchanged(far, "phi", top)
    scale = PHI ** -0.5

    def edge(a, b):
        return (keep[a:b, :mode_rows] + recv[a:b, :mode_rows] + far[a:b].astype(F32)) * scale

    before = moved(edge(depth - SWEEPS, depth), "gz", 1)
    after = moved(edge(0, SWEEPS), "gz", -1)
    own_orders = row_orders[:mode_rows].astype(F32)[:, None]
    potential, shift, totals = solve(keep, recv, far, before, after, open_wide, own_orders, total_depth)
    incoming = later_sum(totals, "gz")
    pieces = [(shift + incoming[None]).astype(BF16)]
    bit = top
    while bit:
        pieces = pieces + [exchanged(piece, "phi", bit) for piece in pieces]
        bit //= 2
    distortion = synthesise(pieces, weights)
    return distortion, potential


def solution(mesh):
    return jax.shard_map(
        on_device,
        mesh=mesh,
        in_specs=(P(("grp", "phi"), "gz", None), P(), P("gz", None)),
        out_specs=(P(("grp", "phi"), "gz", None), P(("grp", "phi"), "gz", None)),
        check_vma=False,
    )
```
